256 devices in a mesh: wide: 32 (over y, z), narrow: 8 (over x, core).
Axes of the slice: x: 4, y: 4, z: 8, core: 2. Of those that a mesh axis runs over, the one named last changes fastest.
Arguments:
- displacement: float32 [32, 8, 2048, 128], P('wide', 'narrow'), may hold values from -6 to 6
- applied_loads: float32 [32, 8, 2048, 128], P('wide', 'narrow'), may hold values from -6 to 6
- stiff_blocks: bfloat16 [32, 8, 16, 7, 128, 128], P('wide', 'narrow'), may hold values from -0.1875 to 0.1875
- stiff_columns: int32 [32, 8, 16, 7], P('wide', 'narrow'), may hold values from 0 to 15, all different within a row
- face_rows: int32 [32, 8, 2, 256], P('wide', 'narrow'), may hold values from 0 to 2047, as said below
- coupling: bfloat16 [32, 8, 2, 256, 256], P('wide', 'narrow'), may hold values from -0.375 to 0.375
- inverse_blocks: bfloat16 [32, 8, 16, 8, 128, 128], P('wide', 'narrow'), may hold values from -0.09375 to 0.09375
- inverse_columns: int32 [32, 8, 16, 8], P('wide', 'narrow'), may hold values from 0 to 15, all different within a row
Outputs:
- solution: float32 [32, 8, 2048, 128], P('wide', 'narrow')
- last_residual: float32 [32, 8, 2048, 128], P('wide', 'narrow')
The draws below stay inside these ranges and needn't reach their ends.
Inputs may be any that keep to these rules, and one draw needn't show every extreme that they name: `stiff_columns`: within each block row the 7 column blocks are distinct. `inverse_columns`: within each block row the 8 coefficient blocks are distinct. `face_rows`: on each subdomain the 512 listed rows are distinct; entry 0 lists the rows of the lower face, entry 1 those of the upper face.
All inputs are finite; a program needn't handle non-finite values.
Results may differ from the reference program's by a relative error of at most 0.003.
Values may be sent and summed in bfloat16 or wider, within the bound.
No kernel may reach another device: no remote copies, remote signals or barrier semaphores. Data moves between devices by JAX's collectives and lax.ppermute only.
A program may use at most 128 MiB of HBM per device.

```python
import jax
import jax.numpy as jnp
from jax import lax

LOADS = 128
BLK = 128
ROWS = 2048
FACE = 256
KNZ = 7
XNZ = 8
SEPL = 256
ITERS = 2
NB = 16
CB = 16
N_WIDE = 32
N_NARROW = 8


def draw_face_rows(key, part):
    device_count = N_WIDE * N_NARROW
    keys = jax.random.split(key, device_count)
    numbers = jnp.arange(device_count, dtype=jnp.int32)

    def one_device(subkey, number):
        first, second, third = jax.random.split(subkey, 3)
        drawn = jax.random.permutation(first, ROWS).astype(jnp.int32)[:2 * FACE]
        inner = (jax.random.permutation(second, ROWS - 2) + 1).astype(jnp.int32)
        forced = jnp.concatenate([jnp.array([0, ROWS - 1], jnp.int32), inner[:2 * FACE - 2]])
        forced = jax.random.permutation(third, forced).astype(jnp.int32)
        return jnp.where(number == 0, forced, drawn)
    chosen = jax.vmap(one_device)(keys, numbers)
    return chosen.reshape(N_WIDE, N_NARROW, 2, FACE)


def steps_of(own_key, dims, cuts, smallest, high):
    factor_of = 1.0
    for axis_at, shards_of in cuts:
        heights = jax.random.uniform(jax.random.fold_in(jax.random.fold_in(own_key, 6), axis_at), (shards_of,), jnp.float32, smallest / len(cuts), high / len(cuts))
        factor_of = factor_of * jnp.repeat(jnp.exp(heights), dims[axis_at] // shards_of).reshape((-1,) + (1,) * (len(dims) - 1 - axis_at))
    return factor_of


def picks_of(own_key, rows, count, top, lift):
    ranking = jax.random.permutation(jax.random.fold_in(own_key, 1), count)
    boost = ranking
    for power in range(3):
        boost = boost * boost // count
    boost = boost * lift // count
    lots = jax.random.randint(jax.random.fold_in(own_key, 2), (rows, count), 0, 4096) + boost
    fixed_rows = jax.random.permutation(jax.random.fold_in(own_key, 3), rows)[jnp.arange(count) % rows]
    lots = jnp.where(jnp.arange(rows)[:, None] == fixed_rows[None, :], 1 << 14, lots)
    score = lots * count + jnp.arange(count)
    return lax.top_k(score.astype(jnp.int32), top)[1].astype(jnp.int32)


def noise(key, shape, deviation, most, cuts=(), held_as=jnp.bfloat16):
    result = jax.random.normal(key, shape, jnp.float32) * deviation
    if len(cuts) > 0:
        result = steps_of(key, shape, cuts, -0.22, 0.18) * result
    return jnp.clip(result, min=-most, max=most).astype(held_as)


def setup_inputs(seed: int = 0) -> dict:
    key_of = jax.random.split(jax.random.key(seed), 9)
    displacement = noise(key_of[0], (N_WIDE, N_NARROW, ROWS, LOADS), 1.0, 6.0, ((0, 32), (1, 8)), jnp.float32)
    applied_loads = noise(key_of[1], (N_WIDE, N_NARROW, ROWS, LOADS), 1.0, 6.0, ((0, 32), (1, 8)), jnp.float32)
    stiff_blocks = noise(key_of[2], (N_WIDE, N_NARROW, NB, KNZ, BLK, BLK), (KNZ * BLK) ** -0.5, 0.1875, ((0, 32), (1, 8)))
    stiff_columns = picks_of(key_of[3], N_WIDE * N_NARROW * NB, NB, KNZ, 0).reshape((N_WIDE, N_NARROW, NB, KNZ))
    face_rows = draw_face_rows(jax.random.fold_in(key_of[8], 71), 0)
    coupling = noise(key_of[5], (N_WIDE, N_NARROW, 2, FACE, FACE), FACE ** -0.5, 0.375, ((0, 32), (1, 8)))
    inverse_blocks = noise(key_of[6], (N_WIDE, N_NARROW, NB, XNZ, BLK, BLK), (4 * XNZ * BLK) ** -0.5, 0.09375, ((0, 32), (1, 8)))
    inverse_columns = picks_of(key_of[7], N_WIDE * N_NARROW * NB, CB, XNZ, 0).reshape((N_WIDE, N_NARROW, NB, XNZ))
    return dict(displacement=displacement, applied_loads=applied_loads, stiff_blocks=stiff_blocks, stiff_columns=stiff_columns, face_rows=face_rows, coupling=coupling, inverse_blocks=inverse_blocks, inverse_columns=inverse_columns)


def bits_of(count):
    return count.bit_length() - 1


def block_product(mats, picked):
    return jnp.einsum("ijab,ijbc->iac", mats.astype(jnp.float32), picked.astype(jnp.float32))


def residual_part(current_b, applied, stiff_mat, stiff_index, face_list, couple, from_below, from_above):
    row_count, load_count = current_b.shape
    block_size = stiff_mat.shape[-1]
    blocks = current_b.reshape(row_count // block_size, block_size, load_count)
    product = block_product(stiff_mat, blocks[stiff_index]).reshape(row_count, load_count)
    lower = jnp.dot(couple[0], from_below, preferred_element_type=jnp.float32)
    upper = jnp.dot(couple[1], from_above, preferred_element_type=jnp.float32)
    residual = applied - product
    residual = residual.at[face_list[0]].add(-lower)
    residual = residual.at[face_list[1]].add(-upper)
    return residual


def coefficient_part(residual_b, inverse_mat, inverse_index, column_blocks):
    block_count, width, block_size, _ = inverse_mat.shape
    blocks = residual_b.reshape(block_count, block_size, -1)
    terms = jnp.einsum("ijab,iac->ijbc", inverse_mat.astype(jnp.float32), blocks.astype(jnp.float32))
    terms = terms.reshape(block_count * width, block_size, -1)
    return jax.ops.segment_sum(terms, inverse_index.reshape(-1), num_segments=column_blocks)


def update_part(coeff_b, inverse_mat, inverse_index):
    return block_product(inverse_mat, coeff_b[inverse_index]).reshape(-1, coeff_b.shape[-1])


def reference(displacement, applied_loads, stiff_blocks, stiff_columns, face_rows, coupling, inverse_blocks, inverse_columns):
    device_count = N_WIDE * N_NARROW
    level_count = bits_of(N_WIDE) + bits_of(N_NARROW)
    column_blocks = level_count * SEPL // BLK

    def flatten(array):
        return array.reshape((device_count,) + array.shape[2:])

    current = flatten(displacement)
    applied = flatten(applied_loads)
    stiff_mat = flatten(stiff_blocks)
    stiff_index = flatten(stiff_columns)
    face_list = flatten(face_rows)
    couple = flatten(coupling)
    inverse_mat = flatten(inverse_blocks)
    inverse_index = flatten(inverse_columns)
    scale = jnp.exp2(-(jnp.arange(level_count).astype(jnp.float32) + 1.0) * 0.5)

    def pick_rows(values, rows_list):
        return values[rows_list]

    residual = applied
    for sweep in range(ITERS):
        current_b = current.astype(jnp.bfloat16)
        low_vals = jax.vmap(pick_rows)(current_b, face_list[:, 0])
        high_vals = jax.vmap(pick_rows)(current_b, face_list[:, 1])
        low_grid = low_vals.reshape(N_WIDE, N_NARROW, FACE, LOADS)
        high_grid = high_vals.reshape(N_WIDE, N_NARROW, FACE, LOADS)
        zero_rim = jnp.zeros((N_WIDE, 1, FACE, LOADS), current_b.dtype)
        from_below = jnp.concatenate([zero_rim, high_grid[:, :-1]], axis=1).reshape(device_count, FACE, LOADS)
        from_above = jnp.concatenate([low_grid[:, 1:], zero_rim], axis=1).reshape(device_count, FACE, LOADS)

        def residual_one(inputs):
            return residual_part(*inputs)

        residual = lax.map(residual_one, (current_b, applied, stiff_mat, stiff_index, face_list, couple, from_below, from_above))
        residual_b = residual.astype(jnp.bfloat16)

        def coefficient_one(inputs):
            return coefficient_part(inputs[0], inputs[1], inputs[2], column_blocks)

        partial_value = lax.map(coefficient_one, (residual_b, inverse_mat, inverse_index))
        partial_value = partial_value.reshape(device_count, level_count, SEPL, LOADS)
        summed = []
        for level in range(level_count):
            group = 2 ** (level + 1)
            grouped = partial_value[:, level].reshape(device_count // group, group, SEPL, LOADS).sum(axis=1)
            summed.append(jnp.repeat(grouped, group, axis=0))
        coeff = jnp.stack(summed, axis=1) * scale[None, :, None, None]
        coeff_b = coeff.astype(jnp.bfloat16).reshape(device_count, column_blocks, BLK, LOADS)

        def update_one(inputs):
            return update_part(*inputs)

        update = lax.map(update_one, (coeff_b, inverse_mat, inverse_index))
        current = current + update
    solution = current.reshape(N_WIDE, N_NARROW, ROWS, LOADS)
    last_residual = residual.reshape(N_WIDE, N_NARROW, ROWS, LOADS)
    return (solution, last_residual)
```

```python
import functools

import jax
import jax.numpy as jnp
from jax import lax
from jax.experimental import pallas as pl
from jax.experimental.pallas import tpu as pltpu
from jax.sharding import PartitionSpec as P

ITERS = 2
BLK = 128
NB = 16
KNZ = 7
XNZ = 8
FACE = 256
LEVELS = 8
GROUP = 4
SLICES = 8
PIECE = 2 * (BLK // SLICES)

bf16 = jnp.bfloat16
f32 = jnp.float32
VMEM = pltpu.VMEM
SMEM = pltpu.SMEM


def gather_rows(cur_ref, face_ref, rows_ref, low_ref, high_ref):
    def body(t, _):
        base = t * 16
        for k in range(16):
            rows_ref[pl.ds(base + k, 1), :] = cur_ref[pl.ds(face_ref[base + k], 1), :]
        return 0

    lax.fori_loop(0, 2 * FACE // 16, body, 0)
    low_ref[...] = rows_ref[0:FACE, :].astype(bf16)
    high_ref[...] = rows_ref[FACE : 2 * FACE, :].astype(bf16)


def faces_kernel(face_ref, cur_ref, low_ref, high_ref, rows_ref):
    gather_rows(cur_ref, face_ref, rows_ref, low_ref, high_ref)


def product_kernel(cols_ref, stiff_ref, cur_ref, applied_ref, out_ref, curb_ref):
    g = pl.program_id(0)

    @pl.when(g == 0)
    def _():
        curb_ref[...] = cur_ref[...].astype(bf16).reshape(NB, BLK, BLK)

    for ii in range(GROUP):
        row = (g * GROUP + ii) * KNZ
        mats = jnp.concatenate([stiff_ref[ii, j] for j in range(KNZ)], axis=1)
        picked = jnp.concatenate([curb_ref[cols_ref[row + j]] for j in range(KNZ)], axis=0)
        prod = jnp.dot(mats, picked, preferred_element_type=f32)
        out_ref[ii * BLK : (ii + 1) * BLK, :] = applied_ref[ii * BLK : (ii + 1) * BLK, :] - prod


def partial_kernel(
    cols_ref, face_ref, me_ref, inv_ref, base_ref, below_ref, above_ref, couple_ref,
    res_ref, keep_ref, send_ref, side_ref, acc_ref,
):
    g = pl.program_id(0)

    @pl.when(g == 0)
    def _():
        res_ref[...] = base_ref[...]
        side_ref[0:FACE, :] = jnp.dot(couple_ref[0], below_ref[...], preferred_element_type=f32)
        side_ref[FACE : 2 * FACE, :] = jnp.dot(
            couple_ref[1], above_ref[...], preferred_element_type=f32
        )

        def body(t, _):
            first = t * 16
            rows = [face_ref[first + k] for k in range(16)]
            olds = [res_ref[pl.ds(rows[k], 1), :] for k in range(16)]
            for k in range(16):
                res_ref[pl.ds(rows[k], 1), :] = olds[k] - side_ref[pl.ds(first + k, 1), :]
            return 0

        lax.fori_loop(0, 2 * FACE // 16, body, 0)
        acc_ref[...] = jnp.zeros_like(acc_ref)

    for ii in range(GROUP):
        i = g * GROUP + ii
        block = res_ref[pl.ds(pl.multiple_of(i * BLK, BLK), BLK), :].astype(bf16)
        mats = jnp.concatenate([inv_ref[ii, j] for j in range(XNZ)], axis=1)
        terms = jnp.dot(block.T, mats, preferred_element_type=f32)
        for j in range(XNZ):
            acc_ref[cols_ref[i * XNZ + j]] += terms[:, j * BLK : (j + 1) * BLK]

    @pl.when(g == NB // GROUP - 1)
    def _():
        me = me_ref[0]
        half = PIECE // 2
        for rel in range(SLICES):
            start = pl.multiple_of((me ^ rel) * half, half)
            for c in range(NB):
                level, h = divmod(c, 2)
                value = acc_ref[c, pl.ds(start, half), :]
                if rel < SLICES // 2:
                    keep_ref[rel, level, h * half : (h + 1) * half, :] = value
                else:
                    send_ref[rel - SLICES // 2, level, h * half : (h + 1) * half, :] = value.astype(
                        bf16
                    )


def update_kernel(gather, cols_ref, face_ref, me_ref, inv_ref, own_ref, got_ref, cur_ref, *rest):
    if gather:
        new_ref, low_ref, high_ref, coeff_ref, rows_ref = rest
    else:
        new_ref, coeff_ref = rest
    g = pl.program_id(0)

    @pl.when(g == 0)
    def _():
        me = me_ref[0]
        half = PIECE // 2
        for rel in range(SLICES):
            start = pl.multiple_of((me ^ rel) * half, half)
            src = own_ref if rel < SLICES // 2 else got_ref
            for c in range(NB):
                level, h = divmod(c, 2)
                coeff_ref[c, pl.ds(start, half), :] = src[
                    rel % (SLICES // 2), level, h * half : (h + 1) * half, :
                ]

    for ii in range(GROUP):
        i = g * GROUP + ii
        mats = jnp.concatenate([inv_ref[ii, j] for j in range(XNZ)], axis=1)
        picked = jnp.concatenate([coeff_ref[cols_ref[i * XNZ + j]] for j in range(XNZ)], axis=1)
        upd = lax.dot_general(mats, picked, (((1,), (1,)), ((), ())), preferred_element_type=f32)
        rows = pl.ds(pl.multiple_of(i * BLK, BLK), BLK)
        new_ref[rows, :] = cur_ref[rows, :] + upd

    if gather:

        @pl.when(g == NB // GROUP - 1)
        def _():
            gather_rows(new_ref, face_ref, rows_ref, low_ref, high_ref)


def sds(shape, dtype):
    return jax.ShapeDtypeStruct(shape, dtype)


def whole(shape):
    return pl.BlockSpec(shape, lambda g, *_: (0,) * len(shape))


ROWS = NB * BLK
STEPS = NB // GROUP
KEEP = (SLICES // 2, LEVELS, PIECE, BLK)


def faces_of(cur, faces):
    return pl.pallas_call(
        faces_kernel,
        grid_spec=pltpu.PrefetchScalarGridSpec(
            num_scalar_prefetch=1,
            grid=(1,),
            in_specs=[whole((ROWS, BLK))],
            out_specs=[whole((FACE, BLK))] * 2,
            scratch_shapes=[VMEM((2 * FACE, BLK), f32)],
        ),
        out_shape=[sds((FACE, BLK), bf16)] * 2,
        name="faces",
    )(faces, cur)


def base_of(cur, applied, stiff, cols):
    return pl.pallas_call(
        product_kernel,
        grid_spec=pltpu.PrefetchScalarGridSpec(
            num_scalar_prefetch=1,
            grid=(STEPS,),
            in_specs=[
                pl.BlockSpec((GROUP, KNZ, BLK, BLK), lambda g, *_: (g, 0, 0, 0)),
                whole((ROWS, BLK)),
                pl.BlockSpec((GROUP * BLK, BLK), lambda g, *_: (g, 0)),
            ],
            out_specs=pl.BlockSpec((GROUP * BLK, BLK), lambda g, *_: (g, 0)),
            scratch_shapes=[VMEM((NB, BLK, BLK), bf16)],
        ),
        out_shape=sds((ROWS, BLK), f32),
        cost_estimate=pl.CostEstimate(
            flops=2 * NB * KNZ * BLK**3, bytes_accessed=8_000_000, transcendentals=0
        ),
        name="product",
    )(cols, stiff, cur, applied)


def partial_of(base, below, above, couple, inverse, cols, faces, me):
    return pl.pallas_call(
        partial_kernel,
        grid_spec=pltpu.PrefetchScalarGridSpec(
            num_scalar_prefetch=3,
            grid=(STEPS,),
            in_specs=[
                pl.BlockSpec((GROUP, XNZ, BLK, BLK), lambda g, *_: (g, 0, 0, 0)),
                whole((ROWS, BLK)),
                whole((FACE, BLK)),
                whole((FACE, BLK)),
                whole((2, FACE, FACE)),
            ],
            out_specs=[whole((ROWS, BLK)), whole(KEEP), whole(KEEP)],
            scratch_shapes=[VMEM((2 * FACE, BLK), f32), VMEM((NB, BLK, BLK), f32)],
        ),
        out_shape=[sds((ROWS, BLK), f32), sds(KEEP, f32), sds(KEEP, bf16)],
        cost_estimate=pl.CostEstimate(
            flops=2 * NB * XNZ * BLK**3, bytes_accessed=8_000_000, transcendentals=0
        ),
        name="partial",
    )(cols, faces, me, inverse, base, below, above, couple)


def update_of(own, got, cur, inverse, cols, faces, me, gather):
    scratch = [VMEM((NB, BLK, BLK), bf16)]
    outs, specs = [sds((ROWS, BLK), f32)], [whole((ROWS, BLK))]
    if gather:
        scratch.append(VMEM((2 * FACE, BLK), f32))
        outs += [sds((FACE, BLK), bf16)] * 2
        specs += [whole((FACE, BLK))] * 2
    return pl.pallas_call(
        functools.partial(update_kernel, gather),
        grid_spec=pltpu.PrefetchScalarGridSpec(
            num_scalar_prefetch=3,
            grid=(STEPS,),
            in_specs=[
                pl.BlockSpec((GROUP, XNZ, BLK, BLK), lambda g, *_: (g, 0, 0, 0)),
                whole(KEEP),
                whole(KEEP),
                whole((ROWS, BLK)),
            ],
            out_specs=specs,
            scratch_shapes=scratch,
        ),
        out_shape=outs,
        cost_estimate=pl.CostEstimate(
            flops=2 * NB * XNZ * BLK**3, bytes_accessed=8_000_000, transcendentals=0
        ),
        name="update",
    )(cols, faces, me, inverse, own, got, cur)


def swapped(value, axis, mask):
    return lax.ppermute(value, axis, [(i, i ^ mask) for i in range(lax.axis_size(axis))])


def shifted(value, steps):
    count = lax.axis_size("narrow")
    pairs = [(i, i + steps) for i in range(count) if 0 <= i + steps < count]
    return lax.ppermute(value, "narrow", pairs)


def rounded(total, level):
    return (total * f32(2.0 ** (-level / 2))).astype(bf16)


def summed(keep, send):
    done = {}
    total = keep + swapped(send, "narrow", 1).astype(f32)
    done[1] = rounded(total[:, :1], 1)
    for level, mask in ((2, 2), (3, 6)):
        size = total.shape[0] // 2
        got = swapped(total[size:, 1:].astype(bf16), "narrow", mask)
        total = total[:size, 1:] + got.astype(f32)
        done[level] = rounded(total[:, :1], level)
    for level, mask in ((4, 1), (5, 2), (6, 6), (7, 8), (8, 24)):
        total = total[:, 1:]
        total = total + swapped(total.astype(bf16), "wide", mask).astype(f32)
        done[level] = rounded(total[:, :1], level)
    mine = jnp.concatenate([done[level] for level in range(3, LEVELS + 1)], axis=1)
    for level, mask in ((2, 6), (1, 2)):
        mine = jnp.concatenate([mine, swapped(mine, "narrow", mask)], axis=0)
        mine = jnp.concatenate([done[level], mine], axis=1)
    return mine, swapped(mine, "narrow", 1)


def per_device(
    displacement, applied_loads, stiff_blocks, stiff_columns,
    face_rows, coupling, inverse_blocks, inverse_columns,
):
    current = displacement[0, 0]
    applied = applied_loads[0, 0]
    stiff = stiff_blocks[0, 0]
    stiff_cols = stiff_columns[0, 0].reshape(-1)
    faces = face_rows[0, 0].reshape(-1)
    couple = coupling[0, 0]
    inverse = inverse_blocks[0, 0]
    inverse_cols = inverse_columns[0, 0].reshape(-1)
    place = lax.axis_index("narrow").astype(jnp.int32)
    core, bit0, bit1 = place & 1, (place >> 1) & 1, (place >> 2) & 1
    me = (core * 4 + (bit0 ^ bit1) * 2 + bit1).reshape(1)
    low, high = faces_of(current, faces)
    for sweep in range(ITERS):
        below = shifted(high, 1)
        above = shifted(low, -1)
        base = base_of(current, applied, stiff, stiff_cols)
        residual, keep, send = partial_of(
            base, below, above, couple, inverse, inverse_cols, faces, me
        )
        own, got = summed(keep, send)
        last = sweep == ITERS - 1
        outs = update_of(own, got, current, inverse, inverse_cols, faces, me, not last)
        current = outs[0]
        if not last:
            low, high = outs[1:]
    return (current[None, None], residual[None, None])


def solution(mesh):
    placed = (
        P("wide", "narrow", None, None),
        P("wide", "narrow", None, None),
        P("wide", "narrow", None, None, None, None),
        P("wide", "narrow", None, None),
        P("wide", "narrow", None, None),
        P("wide", "narrow", None, None, None),
        P("wide", "narrow", None, None, None, None),
        P("wide", "narrow", None, None),
    )
    return jax.shard_map(
        per_device,
        mesh=mesh,
        in_specs=placed,
        out_specs=(P("wide", "narrow", None, None), P("wide", "narrow", None, None)),
        check_vma=False,
    )
```

```python
import functools

import jax
import jax.numpy as jnp
from jax import lax
from jax.experimental import pallas as pl
from jax.experimental.pallas import tpu as pltpu
from jax.sharding import PartitionSpec as P

ITERS = 2
BLK = 128
NB = 16
KNZ = 7
XNZ = 8
FACE = 256
LEVELS = 8
GROUP = 4
SLICES = 4
HALF = BLK // SLICES
PIECE = 2 * HALF

LIMIT = 20 * 2**20

bf16 = jnp.bfloat16
f32 = jnp.float32
VMEM = pltpu.VMEM
SMEM = pltpu.SMEM


def gather_rows(cur_ref, face_ref, place_ref, rows_ref, inner_ref, outer_ref):
    core = place_ref[0]

    def body(t, _):
        base = t * 16
        source = jnp.where(t < FACE // 16, base + (1 - core) * FACE, base - FACE + core * FACE)
        for k in range(16):
            rows_ref[pl.ds(base + k, 1), :] = cur_ref[pl.ds(face_ref[source + k], 1), :]
        return 0

    lax.fori_loop(0, 2 * FACE // 16, body, 0)
    inner_ref[...] = rows_ref[0:FACE, :].astype(bf16)
    outer_ref[...] = rows_ref[FACE : 2 * FACE, :].astype(bf16)


def faces_kernel(face_ref, place_ref, cur_ref, inner_ref, outer_ref, rows_ref):
    gather_rows(cur_ref, face_ref, place_ref, rows_ref, inner_ref, outer_ref)


def product_kernel(cols_ref, stiff_ref, cur_ref, applied_ref, out_ref, curb_ref):
    g = pl.program_id(0)

    @pl.when(g == 0)
    def _():
        curb_ref[...] = cur_ref[...].astype(bf16).reshape(NB, BLK, BLK)

    for ii in range(GROUP):
        row = (g * GROUP + ii) * KNZ
        mats = jnp.concatenate([stiff_ref[ii, j] for j in range(KNZ)], axis=1)
        picked = jnp.concatenate([curb_ref[cols_ref[row + j]] for j in range(KNZ)], axis=0)
        prod = jnp.dot(mats, picked, preferred_element_type=f32)
        out_ref[ii * BLK : (ii + 1) * BLK, :] = applied_ref[ii * BLK : (ii + 1) * BLK, :] - prod


def partial_kernel(
    cols_ref, face_ref, place_ref, inv_ref, base_ref, inner_ref, outer_ref, couple_ref,
    res_ref, keep_ref, send_ref, side_ref, acc_ref,
):
    g = pl.program_id(0)

    @pl.when(g == 0)
    def _():
        res_ref[...] = base_ref[...]
        core = place_ref[0]
        inner = inner_ref[...]
        outer = jnp.where(place_ref[2] != 0, outer_ref[...], jnp.zeros_like(inner))
        for face, got in ((1 - core, inner), (core, outer)):
            side_ref[pl.ds(pl.multiple_of(face * FACE, FACE), FACE), :] = jnp.dot(
                couple_ref[face], got, preferred_element_type=f32
            )

        def body(t, _):
            first = t * 16
            rows = [face_ref[first + k] for k in range(16)]
            olds = [res_ref[pl.ds(rows[k], 1), :] for k in range(16)]
            for k in range(16):
                res_ref[pl.ds(rows[k], 1), :] = olds[k] - side_ref[pl.ds(first + k, 1), :]
            return 0

        lax.fori_loop(0, 2 * FACE // 16, body, 0)
        acc_ref[...] = jnp.zeros_like(acc_ref)

    for ii in range(GROUP):
        i = g * GROUP + ii
        block = res_ref[pl.ds(pl.multiple_of(i * BLK, BLK), BLK), :].astype(bf16)
        mats = jnp.concatenate([inv_ref[ii, j] for j in range(XNZ)], axis=1)
        terms = jnp.dot(block.T, mats, preferred_element_type=f32)
        for j in range(XNZ):
            acc_ref[cols_ref[i * XNZ + j]] += terms[:, j * BLK : (j + 1) * BLK]

    @pl.when(g == NB // GROUP - 1)
    def _():
        for rel in range(SLICES):
            start = pl.multiple_of((place_ref[1] ^ rel) * HALF, HALF)
            for c in range(NB):
                level, h = divmod(c, 2)
                value = acc_ref[c, pl.ds(start, HALF), :]
                keep_ref[rel, level, h * HALF : (h + 1) * HALF, :] = value
                send_ref[rel, level, h * HALF : (h + 1) * HALF, :] = value.astype(bf16)


def update_kernel(gather, cols_ref, face_ref, place_ref, inv_ref, own_ref, got_ref, cur_ref, *rest):
    if gather:
        new_ref, low_ref, high_ref, coeff_ref, rows_ref = rest
    else:
        new_ref, coeff_ref = rest
    g = pl.program_id(0)

    @pl.when(g == 0)
    def _():
        def spread(src):
            for rel in range(SLICES):
                start = pl.multiple_of((place_ref[1] ^ rel) * HALF, HALF)
                for c in range(NB):
                    level, h = divmod(c, 2)
                    coeff_ref[c, pl.ds(start, HALF), :] = src[
                        rel, level, h * HALF : (h + 1) * HALF, :
                    ]

        @pl.when(place_ref[0] == 0)
        def _():
            spread(got_ref)

        @pl.when(place_ref[0] != 0)
        def _():
            spread(own_ref)

    for ii in range(GROUP):
        i = g * GROUP + ii
        mats = jnp.concatenate([inv_ref[ii, j] for j in range(XNZ)], axis=1)
        picked = jnp.concatenate([coeff_ref[cols_ref[i * XNZ + j]] for j in range(XNZ)], axis=1)
        upd = lax.dot_general(mats, picked, (((1,), (1,)), ((), ())), preferred_element_type=f32)
        rows = pl.ds(pl.multiple_of(i * BLK, BLK), BLK)
        new_ref[rows, :] = cur_ref[rows, :] + upd

    if gather:

        @pl.when(g == NB // GROUP - 1)
        def _():
            gather_rows(new_ref, face_ref, place_ref, rows_ref, low_ref, high_ref)


def sds(shape, dtype):
    return jax.ShapeDtypeStruct(shape, dtype)


def whole(shape):
    return pl.BlockSpec(shape, lambda g, *_: (0,) * len(shape))


ROWS = NB * BLK
STEPS = NB // GROUP
KEEP = (SLICES, LEVELS, PIECE, BLK)


def faces_of(cur, faces, place):
    return pl.pallas_call(
        faces_kernel,
        grid_spec=pltpu.PrefetchScalarGridSpec(
            num_scalar_prefetch=2,
            grid=(1,),
            in_specs=[whole((ROWS, BLK))],
            out_specs=[whole((FACE, BLK))] * 2,
            scratch_shapes=[VMEM((2 * FACE, BLK), f32)],
        ),
        out_shape=[sds((FACE, BLK), bf16)] * 2,
        compiler_params=pltpu.CompilerParams(vmem_limit_bytes=LIMIT),
        name="faces",
    )(faces, place, cur)


def base_of(cur, applied, stiff, cols):
    return pl.pallas_call(
        product_kernel,
        grid_spec=pltpu.PrefetchScalarGridSpec(
            num_scalar_prefetch=1,
            grid=(STEPS,),
            in_specs=[
                pl.BlockSpec((GROUP, KNZ, BLK, BLK), lambda g, *_: (g, 0, 0, 0)),
                whole((ROWS, BLK)),
                pl.BlockSpec((GROUP * BLK, BLK), lambda g, *_: (g, 0)),
            ],
            out_specs=pl.BlockSpec((GROUP * BLK, BLK), lambda g, *_: (g, 0)),
            scratch_shapes=[VMEM((NB, BLK, BLK), bf16)],
        ),
        out_shape=sds((ROWS, BLK), f32),
        cost_estimate=pl.CostEstimate(
            flops=2 * NB * KNZ * BLK**3, bytes_accessed=8_000_000, transcendentals=0
        ),
        compiler_params=pltpu.CompilerParams(vmem_limit_bytes=LIMIT),
        name="product",
    )(cols, stiff, cur, applied)


def partial_of(base, inner, outer, couple, inverse, cols, faces, place):
    return pl.pallas_call(
        partial_kernel,
        grid_spec=pltpu.PrefetchScalarGridSpec(
            num_scalar_prefetch=3,
            grid=(STEPS,),
            in_specs=[
                pl.BlockSpec((GROUP, XNZ, BLK, BLK), lambda g, *_: (g, 0, 0, 0)),
                whole((ROWS, BLK)),
                whole((FACE, BLK)),
                whole((FACE, BLK)),
                whole((2, FACE, FACE)),
            ],
            out_specs=[whole((ROWS, BLK)), whole(KEEP), whole(KEEP)],
            scratch_shapes=[VMEM((2 * FACE, BLK), f32), VMEM((NB, BLK, BLK), f32)],
        ),
        out_shape=[sds((ROWS, BLK), f32), sds(KEEP, f32), sds(KEEP, bf16)],
        cost_estimate=pl.CostEstimate(
            flops=2 * NB * XNZ * BLK**3, bytes_accessed=8_000_000, transcendentals=0
        ),
        compiler_params=pltpu.CompilerParams(vmem_limit_bytes=LIMIT),
        name="partial",
    )(cols, faces, place, inverse, base, inner, outer, couple)


def update_of(own, got, cur, inverse, cols, faces, place, gather):
    scratch = [VMEM((NB, BLK, BLK), bf16)]
    outs, specs = [sds((ROWS, BLK), f32)], [whole((ROWS, BLK))]
    if gather:
        scratch.append(VMEM((2 * FACE, BLK), f32))
        outs += [sds((FACE, BLK), bf16)] * 2
        specs += [whole((FACE, BLK))] * 2
    return pl.pallas_call(
        functools.partial(update_kernel, gather),
        grid_spec=pltpu.PrefetchScalarGridSpec(
            num_scalar_prefetch=3,
            grid=(STEPS,),
            in_specs=[
                pl.BlockSpec((GROUP, XNZ, BLK, BLK), lambda g, *_: (g, 0, 0, 0)),
                whole(KEEP),
                whole(KEEP),
                whole((ROWS, BLK)),
            ],
            out_specs=specs,
            scratch_shapes=scratch,
        ),
        out_shape=outs,
        cost_estimate=pl.CostEstimate(
            flops=2 * NB * XNZ * BLK**3, bytes_accessed=8_000_000, transcendentals=0
        ),
        compiler_params=pltpu.CompilerParams(vmem_limit_bytes=LIMIT),
        name="update",
    )(cols, faces, place, inverse, own, got, cur)


def moved(value, pairs):
    return lax.ppermute(value, ("wide", "narrow"), pairs)


def swapped(value, wide_mask, narrow_mask):
    wide, narrow = lax.axis_size("wide"), lax.axis_size("narrow")
    other = (8, 0) if narrow_mask else (0, 2)
    pairs = []
    for w in range(wide):
        for n in range(narrow):
            masks = (wide_mask, narrow_mask) if n % 2 else other
            pairs.append((w * narrow + n, (w ^ masks[0]) * narrow + (n ^ masks[1])))
    return moved(value, pairs)


def handed(value):
    count = lax.axis_size("wide") * lax.axis_size("narrow")
    return moved(value, [(i, i ^ 1) for i in range(count)])


def faces_swapped(inner, outer):
    count = lax.axis_size("narrow")
    return (
        lax.ppermute(inner, "narrow", [(i, i ^ 1) for i in range(count)]),
        lax.ppermute(outer, "narrow", [(i, (i + 1 if i % 2 else i - 1) % count) for i in range(count)]),
    )


def rounded(total, level):
    return (total * f32(2.0 ** (-level / 2))).astype(bf16)


def summed(keep, send):
    done = {}
    got = handed(send)
    low, high = ((keep[part], got[part].astype(f32)) for part in (slice(0, 2), slice(2, 4)))
    sent = (high[0][:, 1:] + high[1][:, 1:]).astype(bf16)
    total = low[0] + low[1]
    done[1] = jnp.concatenate(
        [rounded(total[:, :1], 1), rounded(high[0][:, :1] + high[1][:, :1], 1)], axis=0
    )
    for level, mask in ((2, 2), (3, 6)):
        got = swapped(sent, 0, mask).astype(f32)
        total = total[:, 1:] + got
        done[level] = rounded(total[:, :1], level)
        if level == 2:
            sent = total[1:, 1:].astype(bf16)
            total = total[:1]
    for level, mask in ((4, 1), (5, 2), (6, 6), (7, 8), (8, 24)):
        total = total[:, 1:]
        total = total + swapped(total.astype(bf16), mask, 0).astype(f32)
        done[level] = rounded(total[:, :1], level)
    mine = jnp.concatenate([done[level] for level in range(3, LEVELS + 1)], axis=1)
    for level, mask in ((2, 6), (1, 2)):
        mine = jnp.concatenate([mine, swapped(mine, 0, mask)], axis=0)
        mine = jnp.concatenate([done[level], mine], axis=1)
    return mine, handed(mine)


def per_device(
    displacement, applied_loads, stiff_blocks, stiff_columns,
    face_rows, coupling, inverse_blocks, inverse_columns,
):
    current = displacement[0, 0]
    applied = applied_loads[0, 0]
    stiff = stiff_blocks[0, 0]
    stiff_cols = stiff_columns[0, 0].reshape(-1)
    faces = face_rows[0, 0].reshape(-1)
    couple = coupling[0, 0]
    inverse = inverse_blocks[0, 0]
    inverse_cols = inverse_columns[0, 0].reshape(-1)
    number = lax.axis_index("narrow").astype(jnp.int32)
    core, bit0, bit1 = number & 1, (number >> 1) & 1, (number >> 2) & 1
    inside = ((number > 0) & (number < lax.axis_size("narrow") - 1)).astype(jnp.int32)
    place = jnp.stack([core, (bit0 ^ bit1) * 2 + bit1, inside])
    inner, outer = faces_of(current, faces, place)
    for sweep in range(ITERS):
        inner, outer = faces_swapped(inner, outer)
        base = base_of(current, applied, stiff, stiff_cols)
        residual, keep, send = partial_of(
            base, inner, outer, couple, inverse, inverse_cols, faces, place
        )
        own, got = summed(keep, send)
        last = sweep == ITERS - 1
        outs = update_of(own, got, current, inverse, inverse_cols, faces, place, not last)
        current = outs[0]
        if not last:
            inner, outer = outs[1:]
    return (current[None, None], residual[None, None])


def solution(mesh):
    placed = (
        P("wide", "narrow", None, None),
        P("wide", "narrow", None, None),
        P("wide", "narrow", None, None, None, None),
        P("wide", "narrow", None, None),
        P("wide", "narrow", None, None),
        P("wide", "narrow", None, None, None),
        P("wide", "narrow", None, None, None, None),
        P("wide", "narrow", None, None),
    )
    return jax.shard_map(
        per_device,
        mesh=mesh,
        in_specs=placed,
        out_specs=(P("wide", "narrow", None, None), P("wide", "narrow", None, None)),
        check_vma=False,
    )
```

```python
import functools

import jax
import jax.numpy as jnp
from jax import lax
from jax.experimental import pallas as pl
from jax.experimental.pallas import tpu as pltpu
from jax.sharding import PartitionSpec as P

ITERS = 2
BLK = 128
NB = 16
KNZ = 7
XNZ = 8
FACE = 256
LEVELS = 8
GROUP = 4
SLICES = 4
HALF = BLK // SLICES
PIECE = 2 * HALF
Z = 8

LIMIT = 20 * 2**20

bf16 = jnp.bfloat16
f32 = jnp.float32
VMEM = pltpu.VMEM
SMEM = pltpu.SMEM


def gather_rows(cur_ref, face_ref, place_ref, rows_ref, inner_ref, outer_ref):
    core = place_ref[0]

    def body(t, _):
        base = t * 16
        source = jnp.where(t < FACE // 16, base + (1 - core) * FACE, base - FACE + core * FACE)
        for k in range(16):
            rows_ref[pl.ds(base + k, 1), :] = cur_ref[pl.ds(face_ref[source + k], 1), :]
        return 0

    lax.fori_loop(0, 2 * FACE // 16, body, 0)
    inner_ref[...] = rows_ref[0:FACE, :].astype(bf16)
    outer_ref[...] = rows_ref[FACE : 2 * FACE, :].astype(bf16)


def faces_kernel(face_ref, place_ref, cur_ref, inner_ref, outer_ref, rows_ref):
    gather_rows(cur_ref, face_ref, place_ref, rows_ref, inner_ref, outer_ref)


def product_kernel(cols_ref, stiff_ref, cur_ref, applied_ref, out_ref, curb_ref):
    g = pl.program_id(0)

    @pl.when(g == 0)
    def _():
        curb_ref[...] = cur_ref[...].astype(bf16).reshape(NB, BLK, BLK)

    for ii in range(GROUP):
        row = (g * GROUP + ii) * KNZ
        mats = jnp.concatenate([stiff_ref[ii, j] for j in range(KNZ)], axis=1)
        picked = jnp.concatenate([curb_ref[cols_ref[row + j]] for j in range(KNZ)], axis=0)
        prod = jnp.dot(mats, picked, preferred_element_type=f32)
        out_ref[ii * BLK : (ii + 1) * BLK, :] = applied_ref[ii * BLK : (ii + 1) * BLK, :] - prod


def partial_kernel(
    cols_ref, face_ref, place_ref, inv_ref, base_ref, inner_ref, outer_ref, couple_ref,
    res_ref, keep_ref, send_ref, side_ref, acc_ref,
):
    g = pl.program_id(0)

    @pl.when(g == 0)
    def _():
        res_ref[...] = base_ref[...]
        core = place_ref[0]
        inner = inner_ref[...]
        outer = jnp.where(place_ref[2] != 0, outer_ref[...], jnp.zeros_like(inner))
        for face, got in ((1 - core, inner), (core, outer)):
            side_ref[pl.ds(pl.multiple_of(face * FACE, FACE), FACE), :] = jnp.dot(
                couple_ref[face], got, preferred_element_type=f32
            )

        def body(t, _):
            first = t * 16
            rows = [face_ref[first + k] for k in range(16)]
            olds = [res_ref[pl.ds(rows[k], 1), :] for k in range(16)]
            for k in range(16):
                res_ref[pl.ds(rows[k], 1), :] = olds[k] - side_ref[pl.ds(first + k, 1), :]
            return 0

        lax.fori_loop(0, 2 * FACE // 16, body, 0)
        acc_ref[...] = jnp.zeros_like(acc_ref)

    for ii in range(GROUP):
        i = g * GROUP + ii
        block = res_ref[pl.ds(pl.multiple_of(i * BLK, BLK), BLK), :].astype(bf16)
        mats = jnp.concatenate([inv_ref[ii, j] for j in range(XNZ)], axis=1)
        terms = jnp.dot(block.T, mats, preferred_element_type=f32)
        for j in range(XNZ):
            acc_ref[cols_ref[i * XNZ + j]] += terms[:, j * BLK : (j + 1) * BLK]

    @pl.when(g == NB // GROUP - 1)
    def _():
        for rel in range(SLICES):
            start = pl.multiple_of((place_ref[1] ^ rel) * HALF, HALF)
            for c in range(NB):
                level, h = divmod(c, 2)
                value = acc_ref[c, pl.ds(start, HALF), :]
                keep_ref[rel, level, h * HALF : (h + 1) * HALF, :] = value
                send_ref[rel, level, h * HALF : (h + 1) * HALF, :] = value.astype(bf16)


def update_kernel(gather, cols_ref, face_ref, place_ref, inv_ref, own_ref, got_ref, cur_ref, *rest):
    if gather:
        new_ref, low_ref, high_ref, coeff_ref, rows_ref = rest
    else:
        new_ref, coeff_ref = rest
    g = pl.program_id(0)

    @pl.when(g == 0)
    def _():
        def spread(src):
            for rel in range(SLICES):
                start = pl.multiple_of((place_ref[1] ^ rel) * HALF, HALF)
                for c in range(NB):
                    level, h = divmod(c, 2)
                    coeff_ref[c, pl.ds(start, HALF), :] = src[
                        rel, level, h * HALF : (h + 1) * HALF, :
                    ]

        @pl.when(place_ref[0] == 0)
        def _():
            spread(got_ref)

        @pl.when(place_ref[0] != 0)
        def _():
            spread(own_ref)

    for ii in range(GROUP):
        i = g * GROUP + ii
        mats = jnp.concatenate([inv_ref[ii, j] for j in range(XNZ)], axis=1)
        picked = jnp.concatenate([coeff_ref[cols_ref[i * XNZ + j]] for j in range(XNZ)], axis=1)
        upd = lax.dot_general(mats, picked, (((1,), (1,)), ((), ())), preferred_element_type=f32)
        rows = pl.ds(pl.multiple_of(i * BLK, BLK), BLK)
        new_ref[rows, :] = cur_ref[rows, :] + upd

    if gather:

        @pl.when(g == NB // GROUP - 1)
        def _():
            gather_rows(new_ref, face_ref, place_ref, rows_ref, low_ref, high_ref)


def sds(shape, dtype):
    return jax.ShapeDtypeStruct(shape, dtype)


def whole(shape):
    return pl.BlockSpec(shape, lambda g, *_: (0,) * len(shape))


ROWS = NB * BLK
STEPS = NB // GROUP
KEEP = (SLICES, LEVELS, PIECE, BLK)


def faces_of(cur, faces, place):
    return pl.pallas_call(
        faces_kernel,
        grid_spec=pltpu.PrefetchScalarGridSpec(
            num_scalar_prefetch=2,
            grid=(1,),
            in_specs=[whole((ROWS, BLK))],
            out_specs=[whole((FACE, BLK))] * 2,
            scratch_shapes=[VMEM((2 * FACE, BLK), f32)],
        ),
        out_shape=[sds((FACE, BLK), bf16)] * 2,
        compiler_params=pltpu.CompilerParams(vmem_limit_bytes=LIMIT),
        name="faces",
    )(faces, place, cur)


def base_of(cur, applied, stiff, cols):
    return pl.pallas_call(
        product_kernel,
        grid_spec=pltpu.PrefetchScalarGridSpec(
            num_scalar_prefetch=1,
            grid=(STEPS,),
            in_specs=[
                pl.BlockSpec((GROUP, KNZ, BLK, BLK), lambda g, *_: (g, 0, 0, 0)),
                whole((ROWS, BLK)),
                pl.BlockSpec((GROUP * BLK, BLK), lambda g, *_: (g, 0)),
            ],
            out_specs=pl.BlockSpec((GROUP * BLK, BLK), lambda g, *_: (g, 0)),
            scratch_shapes=[VMEM((NB, BLK, BLK), bf16)],
        ),
        out_shape=sds((ROWS, BLK), f32),
        cost_estimate=pl.CostEstimate(
            flops=2 * NB * KNZ * BLK**3, bytes_accessed=8_000_000, transcendentals=0
        ),
        compiler_params=pltpu.CompilerParams(vmem_limit_bytes=LIMIT),
        name="product",
    )(cols, stiff, cur, applied)


def partial_of(base, inner, outer, couple, inverse, cols, faces, place):
    return pl.pallas_call(
        partial_kernel,
        grid_spec=pltpu.PrefetchScalarGridSpec(
            num_scalar_prefetch=3,
            grid=(STEPS,),
            in_specs=[
                pl.BlockSpec((GROUP, XNZ, BLK, BLK), lambda g, *_: (g, 0, 0, 0)),
                whole((ROWS, BLK)),
                whole((FACE, BLK)),
                whole((FACE, BLK)),
                whole((2, FACE, FACE)),
            ],
            out_specs=[whole((ROWS, BLK)), whole(KEEP), whole(KEEP)],
            scratch_shapes=[VMEM((2 * FACE, BLK), f32), VMEM((NB, BLK, BLK), f32)],
        ),
        out_shape=[sds((ROWS, BLK), f32), sds(KEEP, f32), sds(KEEP, bf16)],
        cost_estimate=pl.CostEstimate(
            flops=2 * NB * XNZ * BLK**3, bytes_accessed=8_000_000, transcendentals=0
        ),
        compiler_params=pltpu.CompilerParams(vmem_limit_bytes=LIMIT),
        name="partial",
    )(cols, faces, place, inverse, base, inner, outer, couple)


def update_of(own, got, cur, inverse, cols, faces, place, gather):
    scratch = [VMEM((NB, BLK, BLK), bf16)]
    outs, specs = [sds((ROWS, BLK), f32)], [whole((ROWS, BLK))]
    if gather:
        scratch.append(VMEM((2 * FACE, BLK), f32))
        outs += [sds((FACE, BLK), bf16)] * 2
        specs += [whole((FACE, BLK))] * 2
    return pl.pallas_call(
        functools.partial(update_kernel, gather),
        grid_spec=pltpu.PrefetchScalarGridSpec(
            num_scalar_prefetch=3,
            grid=(STEPS,),
            in_specs=[
                pl.BlockSpec((GROUP, XNZ, BLK, BLK), lambda g, *_: (g, 0, 0, 0)),
                whole(KEEP),
                whole(KEEP),
                whole((ROWS, BLK)),
            ],
            out_specs=specs,
            scratch_shapes=scratch,
        ),
        out_shape=outs,
        cost_estimate=pl.CostEstimate(
            flops=2 * NB * XNZ * BLK**3, bytes_accessed=8_000_000, transcendentals=0
        ),
        compiler_params=pltpu.CompilerParams(vmem_limit_bytes=LIMIT),
        name="update",
    )(cols, faces, place, inverse, own, got, cur)


def moved(value, pairs):
    return lax.ppermute(value, ("wide", "narrow"), pairs)


def sent(value, real, other):
    wide, narrow = lax.axis_size("wide"), lax.axis_size("narrow")
    pairs = []
    for w in range(wide):
        for n in range(narrow):
            to = real(w, n) if n % 2 else other(w, n)
            pairs.append((w * narrow + n, to[0] * narrow + to[1]))
    return moved(value, pairs).astype(f32)


def masked(wide_mask, narrow_mask):
    return lambda w, n: (w ^ wide_mask, n ^ narrow_mask)


def along_z(steps):
    return lambda w, n: (w - w % Z + (w + steps) % Z, n)


X1, X2, X3 = masked(0, 2), masked(0, 4), masked(0, 6)
Z1, Y1, Y2, Y3 = masked(1, 0), masked(8, 0), masked(16, 0), masked(24, 0)


def handed(value):
    count = lax.axis_size("wide") * lax.axis_size("narrow")
    return moved(value, [(i, i ^ 1) for i in range(count)])


def faces_swapped(inner, outer):
    count = lax.axis_size("narrow")
    return (
        lax.ppermute(inner, "narrow", [(i, i ^ 1) for i in range(count)]),
        lax.ppermute(outer, "narrow", [(i, (i + 1 if i % 2 else i - 1) % count) for i in range(count)]),
    )


def rounded(total, level):
    return (total * f32(2.0 ** (-level / 2))).astype(bf16)


def summed(keep, send, spot):
    got = handed(send)

    def pair(slices, levels):
        return keep[slices, levels] + got[slices, levels].astype(f32)

    upper = slice(2, LEVELS)
    near = jnp.concatenate([pair(slice(2, 4), 1), pair(2, upper)], axis=0).astype(bf16)
    near = sent(near, X1, Z1)
    across = sent(pair(1, upper).astype(bf16), X3, Y1)
    far = sent(pair(3, upper).astype(bf16), X2, Y3)
    done1 = rounded(pair(slice(0, SLICES), slice(0, 1)), 1)
    done2 = rounded(pair(slice(0, 2), 1) + near[:2], 2)
    total = pair(0, upper) + near[2:] + across + far
    done3 = rounded(total[:1], 3)

    own = total[1:]
    wire = own.astype(bf16)
    left = sent(wire, along_z(1), X1)
    right = sent(wire, along_z(-1), X3)
    done4 = rounded(own[:1] + jnp.where(spot % 2 == 1, left[:1], right[:1]), 4)
    first, last = spot % 4 == 0, spot % 4 == 3
    own, left, right = own[1:], left[1:], right[1:]
    zero = jnp.zeros_like(own[:1])
    quad = own[:1]
    window = left[1:] + own[1:] + right[1:]
    down = jnp.concatenate([left[:1] + jnp.where(last, quad, zero), window], axis=0)
    up = jnp.concatenate([right[:1] + jnp.where(first, quad, zero), own[1:] + right[1:]], axis=0)
    above = sent(down.astype(bf16), along_z(-3), X1)
    below = sent(up.astype(bf16), along_z(3), X3)
    quad = quad + jnp.where(first, zero, left[:1]) + jnp.where(last, zero, right[:1])
    done5 = rounded(quad + jnp.where(spot % 4 < 2, above[:1], below[:1]), 5)
    total = window + above[1:] + below[1:]
    done6 = rounded(total[:1], 6)

    own = total[1:]
    wire = own.astype(bf16)
    near = sent(wire, Y1, X1)
    across = sent(wire[1:], Y3, X3)
    far = sent(wire[1:], Y2, Z1)
    done7 = rounded(own[:1] + near[:1], 7)
    done8 = rounded(own[1:] + near[1:] + across + far, 8)

    mine = jnp.concatenate([done3, done4, done5, done6, done7, done8], axis=0)
    near = sent(jnp.concatenate([done2, mine], axis=0), X1, Z1).astype(bf16)
    across = sent(mine, X3, Y1).astype(bf16)
    far = sent(mine, X2, Y3).astype(bf16)
    slices = ((done2[:1], mine), (done2[1:], across), (near[:1], near[2:]), (near[1:2], far))
    mine = jnp.stack(
        [jnp.concatenate([done1[r], two, rest], axis=0) for r, (two, rest) in enumerate(slices)]
    )
    return mine, handed(mine)


def per_device(
    displacement, applied_loads, stiff_blocks, stiff_columns,
    face_rows, coupling, inverse_blocks, inverse_columns,
):
    current = displacement[0, 0]
    applied = applied_loads[0, 0]
    stiff = stiff_blocks[0, 0]
    stiff_cols = stiff_columns[0, 0].reshape(-1)
    faces = face_rows[0, 0].reshape(-1)
    couple = coupling[0, 0]
    inverse = inverse_blocks[0, 0]
    inverse_cols = inverse_columns[0, 0].reshape(-1)
    spot = lax.axis_index("wide").astype(jnp.int32) % Z
    number = lax.axis_index("narrow").astype(jnp.int32)
    core, bit0, bit1 = number & 1, (number >> 1) & 1, (number >> 2) & 1
    inside = ((number > 0) & (number < lax.axis_size("narrow") - 1)).astype(jnp.int32)
    place = jnp.stack([core, (bit0 ^ bit1) * 2 + bit1, inside])
    inner, outer = faces_of(current, faces, place)
    for sweep in range(ITERS):
        inner, outer = faces_swapped(inner, outer)
        base = base_of(current, applied, stiff, stiff_cols)
        residual, keep, send = partial_of(
            base, inner, outer, couple, inverse, inverse_cols, faces, place
        )
        own, got = summed(keep, send, spot)
        last = sweep == ITERS - 1
        outs = update_of(own, got, current, inverse, inverse_cols, faces, place, not last)
        current = outs[0]
        if not last:
            inner, outer = outs[1:]
    return (current[None, None], residual[None, None])


def solution(mesh):
    placed = (
        P("wide", "narrow", None, None),
        P("wide", "narrow", None, None),
        P("wide", "narrow", None, None, None, None),
        P("wide", "narrow", None, None),
        P("wide", "narrow", None, None),
        P("wide", "narrow", None, None, None),
        P("wide", "narrow", None, None, None, None),
        P("wide", "narrow", None, None),
    )
    return jax.shard_map(
        per_device,
        mesh=mesh,
        in_specs=placed,
        out_specs=(P("wide", "narrow", None, None), P("wide", "narrow", None, None)),
        check_vma=False,
    )
```

```python
import functools

import jax
import jax.numpy as jnp
from jax import lax
from jax.experimental import pallas as pl
from jax.experimental.pallas import tpu as pltpu
from jax.sharding import PartitionSpec as P

ITERS = 2
BLK = 128
NB = 16
KNZ = 7
XNZ = 8
FACE = 256
LEVELS = 8
GROUP = 4
SLICES = 4
HALF = BLK // SLICES
PIECE = 2 * HALF
Z = 8

LIMIT = 20 * 2**20

bf16 = jnp.bfloat16
f32 = jnp.float32
VMEM = pltpu.VMEM
SMEM = pltpu.SMEM


def gather_rows(cur_ref, face_ref, place_ref, rows_ref, inner_ref, outer_ref):
    core = place_ref[0]

    def body(t, _):
        base = t * 16
        source = jnp.where(t < FACE // 16, base + (1 - core) * FACE, base - FACE + core * FACE)
        for k in range(16):
            rows_ref[pl.ds(base + k, 1), :] = cur_ref[pl.ds(face_ref[source + k], 1), :]
        return 0

    lax.fori_loop(0, 2 * FACE // 16, body, 0)
    inner_ref[...] = rows_ref[0:FACE, :].astype(bf16)
    outer_ref[...] = rows_ref[FACE : 2 * FACE, :].astype(bf16)


def faces_kernel(face_ref, place_ref, cur_ref, inner_ref, outer_ref, curb_ref, rows_ref):
    curb_ref[...] = cur_ref[...].astype(bf16)
    gather_rows(cur_ref, face_ref, place_ref, rows_ref, inner_ref, outer_ref)


def product_kernel(cols_ref, stiff_ref, curb_ref, out_ref):
    g = pl.program_id(0)
    for ii in range(GROUP):
        row = g * GROUP + ii
        mats = jnp.concatenate([stiff_ref[row, j] for j in range(KNZ)], axis=1)
        blocks = [pl.ds(pl.multiple_of(cols_ref[j, row] * BLK, BLK), BLK) for j in range(KNZ)]
        picked = jnp.concatenate([curb_ref[block, :] for block in blocks], axis=0)
        rows = pl.ds(pl.multiple_of(row * BLK, BLK), BLK)
        out_ref[rows, :] = jnp.dot(mats, picked, preferred_element_type=f32)


def partial_kernel(
    last, cols_ref, face_ref, place_ref, inv_ref, applied_ref, prod_ref, inner_ref, outer_ref,
    couple_ref, keep_ref, send_ref, *rest,
):
    if last:
        out_ref, side_ref, acc_ref, res_ref = rest
    else:
        side_ref, acc_ref, res_ref = rest
    g = pl.program_id(0)

    @pl.when(g == 0)
    def _():
        res_ref[...] = applied_ref[...] - prod_ref[...]
        core = place_ref[0]
        inner = inner_ref[...]
        outer = jnp.where(place_ref[2] != 0, outer_ref[...], jnp.zeros_like(inner))
        for face, got in ((1 - core, inner), (core, outer)):
            side_ref[pl.ds(pl.multiple_of(face * FACE, FACE), FACE), :] = jnp.dot(
                couple_ref[face], got, preferred_element_type=f32
            )

        def body(t, _):
            first = t * 16
            rows = [face_ref[first + k] for k in range(16)]
            olds = [res_ref[pl.ds(rows[k], 1), :] for k in range(16)]
            for k in range(16):
                res_ref[pl.ds(rows[k], 1), :] = olds[k] - side_ref[pl.ds(first + k, 1), :]
            return 0

        lax.fori_loop(0, 2 * FACE // 16, body, 0)
        acc_ref[...] = jnp.zeros_like(acc_ref)

    for ii in range(GROUP):
        i = g * GROUP + ii
        block = res_ref[pl.ds(pl.multiple_of(i * BLK, BLK), BLK), :]
        if last:
            out_ref[ii * BLK : (ii + 1) * BLK, :] = block
        block = block.astype(bf16)
        mats = jnp.concatenate([inv_ref[i, j] for j in range(XNZ)], axis=1)
        terms = jnp.dot(block.T, mats, preferred_element_type=f32)
        for j in range(XNZ):
            acc_ref[cols_ref[j, i]] += terms[:, j * BLK : (j + 1) * BLK]

    @pl.when(g == NB // GROUP - 1)
    def _():
        for rel in range(SLICES):
            start = pl.multiple_of((place_ref[1] ^ rel) * HALF, HALF)
            for c in range(NB):
                level, h = divmod(c, 2)
                value = acc_ref[c, pl.ds(start, HALF), :]
                keep_ref[rel, level, h * HALF : (h + 1) * HALF, :] = value
                send_ref[rel, level, h * HALF : (h + 1) * HALF, :] = value.astype(bf16)


def update_kernel(gather, cols_ref, face_ref, place_ref, inv_ref, own_ref, got_ref, cur_ref, *rest):
    if gather:
        new_ref, low_ref, high_ref, curb_ref, coeff_ref, rows_ref = rest
    else:
        new_ref, coeff_ref = rest
    g = pl.program_id(0)

    @pl.when(g == 0)
    def _():
        def spread(src):
            for rel in range(SLICES):
                start = pl.multiple_of((place_ref[1] ^ rel) * HALF, HALF)
                for c in range(NB):
                    level, h = divmod(c, 2)
                    coeff_ref[c, pl.ds(start, HALF), :] = src[
                        rel, level, h * HALF : (h + 1) * HALF, :
                    ]

        @pl.when(place_ref[0] == 0)
        def _():
            spread(got_ref)

        @pl.when(place_ref[0] != 0)
        def _():
            spread(own_ref)

    for ii in range(GROUP):
        i = g * GROUP + ii
        mats = jnp.concatenate([inv_ref[i, j] for j in range(XNZ)], axis=1)
        picked = jnp.concatenate([coeff_ref[cols_ref[j, i]] for j in range(XNZ)], axis=1)
        upd = lax.dot_general(mats, picked, (((1,), (1,)), ((), ())), preferred_element_type=f32)
        rows = pl.ds(pl.multiple_of(i * BLK, BLK), BLK)
        new = cur_ref[rows, :] + upd
        if gather:
            new_ref[rows, :] = new
            curb_ref[rows, :] = new.astype(bf16)
        else:
            new_ref[ii * BLK : (ii + 1) * BLK, :] = new

    if gather:

        @pl.when(g == NB // GROUP - 1)
        def _():
            gather_rows(new_ref, face_ref, place_ref, rows_ref, low_ref, high_ref)


def sds(shape, dtype):
    return jax.ShapeDtypeStruct(shape, dtype)


def resident(count):
    return [pl.BlockSpec(memory_space=VMEM)] * count


ROWS = NB * BLK
STEPS = NB // GROUP
FACES_COST = 60_000_000
KEEP = (SLICES, LEVELS, PIECE, BLK)


STEP_ROWS = pl.BlockSpec((GROUP * BLK, BLK), lambda g, *_: (g, 0))


def call(kernel, name, steps, scalars, inputs, out_shape, out_specs, scratch, cost):
    return pl.pallas_call(
        kernel,
        grid_spec=pltpu.PrefetchScalarGridSpec(
            num_scalar_prefetch=len(scalars),
            grid=(steps,),
            in_specs=resident(len(inputs)),
            out_specs=out_specs,
            scratch_shapes=scratch,
        ),
        out_shape=out_shape,
        cost_estimate=cost,
        compiler_params=pltpu.CompilerParams(vmem_limit_bytes=LIMIT),
        name=name,
    )(*scalars, *inputs)


def cost_of(blocks, moved):
    return pl.CostEstimate(flops=2 * blocks * BLK**3, bytes_accessed=moved, transcendentals=0)


FACE_OUTS = [sds((FACE, BLK), bf16)] * 2 + [sds((ROWS, BLK), bf16)]


def faces_of(cur, faces, place):
    return call(
        faces_kernel, "faces", 1, (faces, place), (cur,), FACE_OUTS, resident(3),
        [VMEM((2 * FACE, BLK), f32)], cost_of(0, FACES_COST),
    )


def product_of(curb, stiff, cols):
    return call(
        product_kernel, "product", STEPS, (cols,), (stiff, curb), [sds((ROWS, BLK), f32)],
        resident(1), [], cost_of(NB * KNZ, 8_000_000),
    )[0]


def partial_of(applied, product, inner, outer, couple, inverse, cols, faces, place, last):
    outs, specs = [sds(KEEP, f32), sds(KEEP, bf16)], resident(2)
    if last:
        outs.append(sds((ROWS, BLK), f32))
        specs.append(STEP_ROWS)
    return call(
        functools.partial(partial_kernel, last), "partial", STEPS, (cols, faces, place),
        (inverse, applied, product, inner, outer, couple), outs, specs,
        [VMEM((2 * FACE, BLK), f32), VMEM((NB, BLK, BLK), f32), VMEM((ROWS, BLK), f32)],
        cost_of(NB * XNZ, 8_000_000),
    )


def update_of(own, got, cur, inverse, cols, faces, place, gather):
    scratch = [VMEM((NB, BLK, BLK), bf16)]
    outs, specs = [sds((ROWS, BLK), f32)], [STEP_ROWS]
    if gather:
        scratch.append(VMEM((2 * FACE, BLK), f32))
        outs += FACE_OUTS
        specs = resident(4)
    return call(
        functools.partial(update_kernel, gather), "update", STEPS, (cols, faces, place),
        (inverse, own, got, cur), outs, specs, scratch, cost_of(NB * XNZ, 8_000_000),
    )


def moved(value, pairs):
    return lax.ppermute(value, ("wide", "narrow"), pairs)


def sent(value, real, other):
    wide, narrow = lax.axis_size("wide"), lax.axis_size("narrow")
    pairs = []
    for w in range(wide):
        for n in range(narrow):
            to = real(w, n) if n % 2 else other(w, n)
            pairs.append((w * narrow + n, to[0] * narrow + to[1]))
    return moved(value, pairs).astype(f32)


def masked(wide_mask, narrow_mask):
    return lambda w, n: (w ^ wide_mask, n ^ narrow_mask)


def along_z(steps):
    return lambda w, n: (w - w % Z + (w + steps) % Z, n)


X1, X2, X3 = masked(0, 2), masked(0, 4), masked(0, 6)
Z1, Y1, Y2, Y3 = masked(1, 0), masked(8, 0), masked(16, 0), masked(24, 0)


def handed(value):
    count = lax.axis_size("wide") * lax.axis_size("narrow")
    return moved(value, [(i, i ^ 1) for i in range(count)])


def faces_swapped(inner, outer):
    count = lax.axis_size("narrow")
    return (
        lax.ppermute(inner, "narrow", [(i, i ^ 1) for i in range(count)]),
        lax.ppermute(outer, "narrow", [(i, (i + 1 if i % 2 else i - 1) % count) for i in range(count)]),
    )


def rounded(total, level):
    return (total * f32(2.0 ** (-level / 2))).astype(bf16)


def summed(keep, send, spot):
    got = handed(send)

    def pair(slices, levels):
        return keep[slices, levels] + got[slices, levels].astype(f32)

    upper = slice(2, LEVELS)
    near = jnp.concatenate([pair(slice(2, 4), 1), pair(2, upper)], axis=0).astype(bf16)
    near = sent(near, X1, Z1)
    across = sent(pair(1, upper).astype(bf16), X3, Y1)
    far = sent(pair(3, upper).astype(bf16), X2, Y3)
    done1 = rounded(pair(slice(0, SLICES), slice(0, 1)), 1)
    done2 = rounded(pair(slice(0, 2), 1) + near[:2], 2)
    total = pair(0, upper) + near[2:] + across + far
    done3 = rounded(total[:1], 3)

    own = total[1:]
    wire = own.astype(bf16)
    left = sent(wire, along_z(1), X1)
    right = sent(wire, along_z(-1), X3)
    done4 = rounded(own[:1] + jnp.where(spot % 2 == 1, left[:1], right[:1]), 4)
    first, last = spot % 4 == 0, spot % 4 == 3
    own, left, right = own[1:], left[1:], right[1:]
    zero = jnp.zeros_like(own[:1])
    quad = own[:1]
    window = left[1:] + own[1:] + right[1:]
    down = jnp.concatenate([left[:1] + jnp.where(last, quad, zero), window], axis=0)
    up = jnp.concatenate([right[:1] + jnp.where(first, quad, zero), own[1:] + right[1:]], axis=0)
    above = sent(down.astype(bf16), along_z(-3), X1)
    below = sent(up.astype(bf16), along_z(3), X3)
    quad = quad + jnp.where(first, zero, left[:1]) + jnp.where(last, zero, right[:1])
    done5 = rounded(quad + jnp.where(spot % 4 < 2, above[:1], below[:1]), 5)
    total = window + above[1:] + below[1:]
    done6 = rounded(total[:1], 6)

    own = total[1:]
    wire = own.astype(bf16)
    near = sent(wire, Y1, X1)
    across = sent(wire[1:], Y3, X3)
    far = sent(wire[1:], Y2, Z1)
    done7 = rounded(own[:1] + near[:1], 7)
    done8 = rounded(own[1:] + near[1:] + across + far, 8)

    mine = jnp.concatenate([done3, done4, done5, done6, done7, done8], axis=0)
    near = sent(jnp.concatenate([done2, mine], axis=0), X1, Z1).astype(bf16)
    across = sent(mine, X3, Y1).astype(bf16)
    far = sent(mine, X2, Y3).astype(bf16)
    slices = ((done2[:1], mine), (done2[1:], across), (near[:1], near[2:]), (near[1:2], far))
    mine = jnp.stack(
        [jnp.concatenate([done1[r], two, rest], axis=0) for r, (two, rest) in enumerate(slices)]
    )
    return mine, handed(mine)


def per_device(
    displacement, applied_loads, stiff_blocks, stiff_columns,
    face_rows, coupling, inverse_blocks, inverse_columns,
):
    current = displacement[0, 0]
    applied = applied_loads[0, 0]
    stiff = stiff_blocks[0, 0]
    stiff_cols = stiff_columns[0, 0].T
    faces = face_rows[0, 0].reshape(-1)
    couple = coupling[0, 0]
    inverse = inverse_blocks[0, 0]
    inverse_cols = inverse_columns[0, 0].T
    spot = lax.axis_index("wide").astype(jnp.int32) % Z
    number = lax.axis_index("narrow").astype(jnp.int32)
    core, bit0, bit1 = number & 1, (number >> 1) & 1, (number >> 2) & 1
    inside = ((number > 0) & (number < lax.axis_size("narrow") - 1)).astype(jnp.int32)
    place = jnp.stack([core, (bit0 ^ bit1) * 2 + bit1, inside])
    inner, outer, rounded_current = faces_of(current, faces, place)
    for sweep in range(ITERS):
        inner, outer = faces_swapped(inner, outer)
        product = product_of(rounded_current, stiff, stiff_cols)
        last = sweep == ITERS - 1
        keep, send, *residual = partial_of(
            applied, product, inner, outer, couple, inverse, inverse_cols, faces, place, last
        )
        own, got = summed(keep, send, spot)
        outs = update_of(own, got, current, inverse, inverse_cols, faces, place, not last)
        current = outs[0]
        if not last:
            inner, outer, rounded_current = outs[1:]
    return (current[None, None], residual[0][None, None])


def solution(mesh):
    placed = (
        P("wide", "narrow", None, None),
        P("wide", "narrow", None, None),
        P("wide", "narrow", None, None, None, None),
        P("wide", "narrow", None, None),
        P("wide", "narrow", None, None),
        P("wide", "narrow", None, None, None),
        P("wide", "narrow", None, None, None, None),
        P("wide", "narrow", None, None),
    )
    return jax.shard_map(
        per_device,
        mesh=mesh,
        in_specs=placed,
        out_specs=(P("wide", "narrow", None, None), P("wide", "narrow", None, None)),
        check_vma=False,
    )
```

```python
import functools

import jax
import jax.numpy as jnp
from jax import lax
from jax.experimental import pallas as pl
from jax.experimental.pallas import tpu as pltpu
from jax.sharding import PartitionSpec as P

ITERS = 2
BLK = 128
NB = 16
KNZ = 7
XNZ = 8
FACE = 256
LEVELS = 8
GROUP = 4
SLICES = 4
HALF = BLK // SLICES
PIECE = 2 * HALF

LIMIT = 20 * 2**20

bf16 = jnp.bfloat16
f32 = jnp.float32
VMEM = pltpu.VMEM
SMEM = pltpu.SMEM


def gather_rows(cur_ref, face_ref, place_ref, rows_ref, inner_ref, outer_ref):
    core = place_ref[0]

    def body(t, _):
        base = t * 16
        source = jnp.where(t < FACE // 16, base + (1 - core) * FACE, base - FACE + core * FACE)
        for k in range(16):
            rows_ref[pl.ds(base + k, 1), :] = cur_ref[pl.ds(face_ref[source + k], 1), :]
        return 0

    lax.fori_loop(0, 2 * FACE // 16, body, 0)
    inner_ref[...] = rows_ref[0:FACE, :].astype(bf16)
    outer_ref[...] = rows_ref[FACE : 2 * FACE, :].astype(bf16)


def faces_kernel(face_ref, place_ref, cur_ref, inner_ref, outer_ref, curb_ref, rows_ref):
    curb_ref[...] = cur_ref[...].astype(bf16)
    gather_rows(cur_ref, face_ref, place_ref, rows_ref, inner_ref, outer_ref)


def product_kernel(cols_ref, stiff_ref, curb_ref, out_ref):
    g = pl.program_id(0)
    for ii in range(GROUP):
        row = g * GROUP + ii
        mats = jnp.concatenate([stiff_ref[row, j] for j in range(KNZ)], axis=1)
        blocks = [pl.ds(pl.multiple_of(cols_ref[j, row] * BLK, BLK), BLK) for j in range(KNZ)]
        picked = jnp.concatenate([curb_ref[block, :] for block in blocks], axis=0)
        rows = pl.ds(pl.multiple_of(row * BLK, BLK), BLK)
        out_ref[rows, :] = jnp.dot(mats, picked, preferred_element_type=f32)


def partial_kernel(
    last, cols_ref, face_ref, place_ref, inv_ref, applied_ref, prod_ref, inner_ref, outer_ref,
    couple_ref, keep_ref, send_ref, *rest,
):
    if last:
        out_ref, side_ref, acc_ref, res_ref = rest
    else:
        side_ref, acc_ref, res_ref = rest
    g = pl.program_id(0)

    @pl.when(g == 0)
    def _():
        res_ref[...] = applied_ref[...] - prod_ref[...]
        core = place_ref[0]
        inner = inner_ref[...]
        outer = jnp.where(place_ref[2] != 0, outer_ref[...], jnp.zeros_like(inner))
        for face, got in ((1 - core, inner), (core, outer)):
            side_ref[pl.ds(pl.multiple_of(face * FACE, FACE), FACE), :] = jnp.dot(
                couple_ref[face], got, preferred_element_type=f32
            )

        def body(t, _):
            first = t * 16
            rows = [face_ref[first + k] for k in range(16)]
            olds = [res_ref[pl.ds(rows[k], 1), :] for k in range(16)]
            for k in range(16):
                res_ref[pl.ds(rows[k], 1), :] = olds[k] - side_ref[pl.ds(first + k, 1), :]
            return 0

        lax.fori_loop(0, 2 * FACE // 16, body, 0)
        acc_ref[...] = jnp.zeros_like(acc_ref)

    for ii in range(GROUP):
        i = g * GROUP + ii
        block = res_ref[pl.ds(pl.multiple_of(i * BLK, BLK), BLK), :]
        if last:
            out_ref[ii * BLK : (ii + 1) * BLK, :] = block
        block = block.astype(bf16)
        mats = jnp.concatenate([inv_ref[i, j] for j in range(XNZ)], axis=1)
        terms = jnp.dot(block.T, mats, preferred_element_type=f32)
        for j in range(XNZ):
            acc_ref[cols_ref[j, i]] += terms[:, j * BLK : (j + 1) * BLK]

    @pl.when(g == NB // GROUP - 1)
    def _():
        for rel in range(SLICES):
            start = pl.multiple_of((place_ref[1] ^ rel) * HALF, HALF)
            for c in range(NB):
                level, h = divmod(c, 2)
                value = acc_ref[c, pl.ds(start, HALF), :]
                keep_ref[rel, level, h * HALF : (h + 1) * HALF, :] = value
                send_ref[rel, level, h * HALF : (h + 1) * HALF, :] = value.astype(bf16)


def update_kernel(gather, cols_ref, face_ref, place_ref, inv_ref, own_ref, got_ref, cur_ref, *rest):
    if gather:
        new_ref, low_ref, high_ref, curb_ref, coeff_ref, rows_ref = rest
    else:
        new_ref, coeff_ref = rest
    g = pl.program_id(0)

    @pl.when(g == 0)
    def _():
        def spread(src):
            for rel in range(SLICES):
                start = pl.multiple_of((place_ref[1] ^ rel) * HALF, HALF)
                for c in range(NB):
                    level, h = divmod(c, 2)
                    coeff_ref[c, pl.ds(start, HALF), :] = src[
                        rel, level, h * HALF : (h + 1) * HALF, :
                    ]

        @pl.when(place_ref[0] == 0)
        def _():
            spread(got_ref)

        @pl.when(place_ref[0] != 0)
        def _():
            spread(own_ref)

    for ii in range(GROUP):
        i = g * GROUP + ii
        mats = jnp.concatenate([inv_ref[i, j] for j in range(XNZ)], axis=1)
        picked = jnp.concatenate([coeff_ref[cols_ref[j, i]] for j in range(XNZ)], axis=1)
        upd = lax.dot_general(mats, picked, (((1,), (1,)), ((), ())), preferred_element_type=f32)
        rows = pl.ds(pl.multiple_of(i * BLK, BLK), BLK)
        new = cur_ref[rows, :] + upd
        if gather:
            new_ref[rows, :] = new
            curb_ref[rows, :] = new.astype(bf16)
        else:
            new_ref[ii * BLK : (ii + 1) * BLK, :] = new

    if gather:

        @pl.when(g == NB // GROUP - 1)
        def _():
            gather_rows(new_ref, face_ref, place_ref, rows_ref, low_ref, high_ref)


def sds(shape, dtype):
    return jax.ShapeDtypeStruct(shape, dtype)


def resident(count):
    return [pl.BlockSpec(memory_space=VMEM)] * count


ROWS = NB * BLK
STEPS = NB // GROUP
FACES_COST = 60_000_000
KEEP = (SLICES, LEVELS, PIECE, BLK)


STEP_ROWS = pl.BlockSpec((GROUP * BLK, BLK), lambda g, *_: (g, 0))


def call(kernel, name, steps, scalars, inputs, out_shape, out_specs, scratch, cost):
    return pl.pallas_call(
        kernel,
        grid_spec=pltpu.PrefetchScalarGridSpec(
            num_scalar_prefetch=len(scalars),
            grid=(steps,),
            in_specs=resident(len(inputs)),
            out_specs=out_specs,
            scratch_shapes=scratch,
        ),
        out_shape=out_shape,
        cost_estimate=cost,
        compiler_params=pltpu.CompilerParams(vmem_limit_bytes=LIMIT),
        name=name,
    )(*scalars, *inputs)


def cost_of(blocks, moved):
    return pl.CostEstimate(flops=2 * blocks * BLK**3, bytes_accessed=moved, transcendentals=0)


FACE_OUTS = [sds((FACE, BLK), bf16)] * 2 + [sds((ROWS, BLK), bf16)]


def faces_of(cur, faces, place):
    return call(
        faces_kernel, "faces", 1, (faces, place), (cur,), FACE_OUTS, resident(3),
        [VMEM((2 * FACE, BLK), f32)], cost_of(0, FACES_COST),
    )


def product_of(curb, stiff, cols):
    return call(
        product_kernel, "product", STEPS, (cols,), (stiff, curb), [sds((ROWS, BLK), f32)],
        resident(1), [], cost_of(NB * KNZ, 8_000_000),
    )[0]


def partial_of(applied, product, inner, outer, couple, inverse, cols, faces, place, last):
    outs, specs = [sds(KEEP, f32), sds(KEEP, bf16)], resident(2)
    if last:
        outs.append(sds((ROWS, BLK), f32))
        specs.append(STEP_ROWS)
    return call(
        functools.partial(partial_kernel, last), "partial", STEPS, (cols, faces, place),
        (inverse, applied, product, inner, outer, couple), outs, specs,
        [VMEM((2 * FACE, BLK), f32), VMEM((NB, BLK, BLK), f32), VMEM((ROWS, BLK), f32)],
        cost_of(NB * XNZ, 8_000_000),
    )


def update_of(own, got, cur, inverse, cols, faces, place, gather):
    scratch = [VMEM((NB, BLK, BLK), bf16)]
    outs, specs = [sds((ROWS, BLK), f32)], [STEP_ROWS]
    if gather:
        scratch.append(VMEM((2 * FACE, BLK), f32))
        outs += FACE_OUTS
        specs = resident(4)
    return call(
        functools.partial(update_kernel, gather), "update", STEPS, (cols, faces, place),
        (inverse, own, got, cur), outs, specs, scratch, cost_of(NB * XNZ, 8_000_000),
    )


def moved(value, pairs):
    return lax.ppermute(value, ("wide", "narrow"), pairs)


def sent(value, real, other):
    wide, narrow = lax.axis_size("wide"), lax.axis_size("narrow")
    pairs = []
    for w in range(wide):
        for n in range(narrow):
            to = real(w, n) if n % 2 else other(w, n)
            pairs.append((w * narrow + n, to[0] * narrow + to[1]))
    return moved(value, pairs).astype(f32)


def masked(wide_mask, narrow_mask):
    return lambda w, n: (w ^ wide_mask, n ^ narrow_mask)


X1, X2, X3 = masked(0, 2), masked(0, 4), masked(0, 6)
Y1, Y2, Y3 = masked(8, 0), masked(16, 0), masked(24, 0)
Z1, Z2, Z6, Z5 = masked(1, 0), masked(2, 0), masked(6, 0), masked(5, 0)


def handed(value):
    count = lax.axis_size("wide") * lax.axis_size("narrow")
    return moved(value, [(i, i ^ 1) for i in range(count)])


def faces_swapped(inner, outer):
    count = lax.axis_size("narrow")
    return (
        lax.ppermute(inner, "narrow", [(i, i ^ 1) for i in range(count)]),
        lax.ppermute(outer, "narrow", [(i, (i + 1 if i % 2 else i - 1) % count) for i in range(count)]),
    )


def rounded(total, level):
    return (total * f32(2.0 ** (-level / 2))).astype(bf16)


def summed(keep, send):
    got = handed(send)

    def pair(slices, levels):
        return keep[slices, levels] + got[slices, levels].astype(f32)

    upper = slice(2, LEVELS)
    near = jnp.concatenate([pair(slice(2, 4), 1), pair(2, upper)], axis=0).astype(bf16)
    near = sent(near, X1, Z1)
    across = sent(pair(1, upper).astype(bf16), X3, Y1)
    far = sent(pair(3, upper).astype(bf16), X2, Y3)
    done1 = rounded(pair(slice(0, SLICES), slice(0, 1)), 1)
    done2 = rounded(pair(slice(0, 2), 1) + near[:2], 2)
    total = pair(0, upper) + near[2:] + across + far
    done3 = rounded(total[:1], 3)

    total = total[1:]
    total = total + sent(total.astype(bf16), Z1, X1)
    done4 = rounded(total[:1], 4)
    wire = total[1:].astype(bf16)
    near = sent(wire, Z2, X1)
    across = sent(wire[1:], Z6, X3)
    far = sent(wire[1:], Z5, Y1)
    total = total[1:] + near
    done5 = rounded(total[:1], 5)
    total = total[1:] + across + far
    done6 = rounded(total[:1], 6)

    own = total[1:]
    wire = own.astype(bf16)
    near = sent(wire, Y1, X1)
    across = sent(wire[1:], Y3, X3)
    far = sent(wire[1:], Y2, Z1)
    done7 = rounded(own[:1] + near[:1], 7)
    done8 = rounded(own[1:] + near[1:] + across + far, 8)

    mine = jnp.concatenate([done3, done4, done5, done6, done7, done8], axis=0)
    near = sent(jnp.concatenate([done2, mine], axis=0), X1, Z1).astype(bf16)
    across = sent(mine, X3, Y1).astype(bf16)
    far = sent(mine, X2, Y3).astype(bf16)
    slices = ((done2[:1], mine), (done2[1:], across), (near[:1], near[2:]), (near[1:2], far))
    mine = jnp.stack(
        [jnp.concatenate([done1[r], two, rest], axis=0) for r, (two, rest) in enumerate(slices)]
    )
    return mine, handed(mine)


def per_device(
    displacement, applied_loads, stiff_blocks, stiff_columns,
    face_rows, coupling, inverse_blocks, inverse_columns,
):
    current = displacement[0, 0]
    applied = applied_loads[0, 0]
    stiff = stiff_blocks[0, 0]
    stiff_cols = stiff_columns[0, 0].T
    faces = face_rows[0, 0].reshape(-1)
    couple = coupling[0, 0]
    inverse = inverse_blocks[0, 0]
    inverse_cols = inverse_columns[0, 0].T
    number = lax.axis_index("narrow").astype(jnp.int32)
    core, bit0, bit1 = number & 1, (number >> 1) & 1, (number >> 2) & 1
    inside = ((number > 0) & (number < lax.axis_size("narrow") - 1)).astype(jnp.int32)
    place = jnp.stack([core, (bit0 ^ bit1) * 2 + bit1, inside])
    inner, outer, rounded_current = faces_of(current, faces, place)
    for sweep in range(ITERS):
        inner, outer = faces_swapped(inner, outer)
        product = product_of(rounded_current, stiff, stiff_cols)
        last = sweep == ITERS - 1
        keep, send, *residual = partial_of(
            applied, product, inner, outer, couple, inverse, inverse_cols, faces, place, last
        )
        own, got = summed(keep, send)
        outs = update_of(own, got, current, inverse, inverse_cols, faces, place, not last)
        current = outs[0]
        if not last:
            inner, outer, rounded_current = outs[1:]
    return (current[None, None], residual[0][None, None])


def solution(mesh):
    placed = (
        P("wide", "narrow", None, None),
        P("wide", "narrow", None, None),
        P("wide", "narrow", None, None, None, None),
        P("wide", "narrow", None, None),
        P("wide", "narrow", None, None),
        P("wide", "narrow", None, None, None),
        P("wide", "narrow", None, None, None, None),
        P("wide", "narrow", None, None),
    )
    return jax.shard_map(
        per_device,
        mesh=mesh,
        in_specs=placed,
        out_specs=(P("wide", "narrow", None, None), P("wide", "narrow", None, None)),
        check_vma=False,
    )
```
